32 devices in a mesh: row: 4 (over y, core), col: 8 (over z, x).
Axes of the slice: x: 2, y: 2, z: 4, core: 2. Of those that a mesh axis runs over, the one named last changes fastest.
Arguments:
- rhs_tile: float32 [18432, 9216], P('row', 'col'), may hold values from -6 to 6
- factor: float32 [18432, 1536], P('row', 'col'), may hold values from -1 to 2.5, as said below
Outputs:
- whitened: float32 [18432, 9216], P('row', 'col')
The draws below stay inside these ranges and needn't reach their ends.
Inputs may be any that keep to these rules, and one draw needn't show every extreme that they name: In elimination order factor is lower triangular: entries above the diagonal are zero, diagonal entries are at least 0.7.
All inputs are finite; a program needn't handle non-finite values.
Results may differ from the reference program's by a relative error of at most 0.0001.
Values sent between devices are 32-bit elements; how exact they have to be, the bound alone decides.
A program may use at most 128 MiB of HBM per device.

```python
import jax
import jax.numpy as jnp
from jax import lax

N = 18432
PANEL = 512
PANELS = 3
ROWS_DEV = 4608
PB = 128
CB = 64
NRHS = 9216


def draw_factor(key, part):
    window = PANELS * PANEL
    stored = jnp.arange(N).astype(jnp.int32)[:, None]
    column = jnp.arange(window).astype(jnp.int32)[None, :]
    local_row = stored % ROWS_DEV
    stored_panel = local_row // PB
    row_rank = jnp.where(stored_panel < PANELS, stored_panel * PANEL + stored // ROWS_DEV * PB + local_row % PB, window + local_row)
    col_owner = column // (PANELS * CB)
    col_local = column % (PANELS * CB)
    col_panel = col_local // CB
    col_rank = col_panel * PANEL + col_owner * CB + col_local % CB
    key_noise = jax.random.fold_in(key, 11)
    key_diag = jax.random.fold_in(key, 23)
    normal_draw = jnp.clip(jax.random.normal(key_noise, (N, window), jnp.float32), -6.0, 6.0)
    diag_vals = jax.random.uniform(key_diag, (N, window), jnp.float32, 1.0, 2.0)
    near_scale = 0.5
    far_scale = 1.0
    same_panel = row_rank // PANEL == col_panel
    lower_vals = jnp.where(same_panel, normal_draw * (near_scale / jnp.sqrt(1.0 * PANEL)), normal_draw * (far_scale / jnp.sqrt(1.0 * window)))
    values = jnp.where(row_rank == col_rank, diag_vals, jnp.where(row_rank > col_rank, lower_vals, 0.0))
    return values.astype(jnp.float32)


def shard_levels(rng, extent, pieces, smallest, largest):
    def one(dim, blocks):
        steps = jax.random.uniform(jax.random.fold_in(jax.random.fold_in(rng, 6), dim), (blocks,), jnp.float32, smallest / len(pieces), largest / len(pieces))
        return jnp.repeat(jnp.exp(steps), extent[dim] // blocks).reshape((-1,) + (1,) * (len(extent) - dim - 1))

    level = one(*pieces[0])
    for cut in pieces[1:]:
        level = level * one(*cut)
    return level


def bell_draw(key, dims, deviation, limit, shards=(), kind=jnp.bfloat16):
    values = deviation * jax.random.normal(key, dims, jnp.float32)
    if shards:
        values = values * shard_levels(key, dims, shards, -0.22, 0.18)
    return jnp.clip(values, -limit, limit).astype(kind)


def setup_inputs(seed: int = 0) -> dict:
    key_of = jax.random.split(jax.random.key(seed), 3)
    rhs_tile = bell_draw(key_of[0], (N, NRHS), 1.0, 6.0, ((0, 4), (1, 8)), jnp.float32)
    factor = draw_factor(jax.random.fold_in(key_of[2], 71), 0)
    return {"rhs_tile": rhs_tile, "factor": factor}


def reference(rhs_tile, factor):
    window = PANELS * PANEL
    index_k = jnp.arange(window).astype(jnp.int32)
    panel_of = index_k // PANEL
    within = index_k % PANEL
    rows_index = (within // PB * ROWS_DEV + panel_of * PB + within % PB).astype(jnp.int32)
    cols_index = (within // CB * (PANELS * CB) + panel_of * CB + within % CB).astype(jnp.int32)
    factor_cols = factor[:, cols_index]
    stored = jnp.arange(N).astype(jnp.int32)
    local_row = stored % ROWS_DEV
    stored_panel = local_row // PB
    order_rank = jnp.where(stored_panel < PANELS, stored_panel * PANEL + stored // ROWS_DEV * PB + local_row % PB, window)
    result = rhs_tile
    for panel_index in range(PANELS):
        start_row = panel_index * PANEL
        end_row = start_row + PANEL
        panel_rows = rows_index[start_row:end_row]
        diagonal = factor_cols[panel_rows][:, start_row:end_row]
        solved = jax.scipy.linalg.solve_triangular(diagonal, result[panel_rows], lower=True)
        update = jnp.dot(factor_cols[:, start_row:end_row].astype(jnp.float32), solved.astype(jnp.float32), precision=lax.Precision.HIGHEST, preferred_element_type=jnp.float32)
        result = jnp.where((order_rank >= end_row)[:, None], result - update, result)
        result = result.at[panel_rows].set(solved)
    return result
```

```python
import functools
import math

import jax
import jax.numpy as jnp
from jax import lax
from jax.experimental import pallas as pl
from jax.experimental.pallas import tpu as pltpu
from jax.sharding import PartitionSpec as P

PANEL = 512
PANELS = 3
HIGHEST = lax.Precision.HIGHEST
MESH = pl.DeviceIdType.MESH


def gather_kernel(outer, inner, tiles, first, rows, own_ref, full_ref, send_sem, recv_sem, local_sem):
    row = lax.axis_index("row")
    col = lax.axis_index("col")
    a, b = lax.div(col, inner), lax.rem(col, inner)
    sides = ((1, 0), (-1, 0), (0, 1), (0, -1))

    def inside(da, db):
        return (a + da >= 0) & (a + da < outer) & (b + db >= 0) & (b + db < inner)

    def place(da, db):
        return (a + da) * inner + b + db

    barrier = pltpu.get_barrier_semaphore()
    for da, db in sides:

        @pl.when(inside(da, db))
        def _(da=da, db=db):
            pl.semaphore_signal(barrier, inc=1, device_id=(row, place(da, db)), device_id_type=MESH)

    peers = sum(inside(da, db).astype(jnp.int32) for da, db in sides)
    pl.semaphore_wait(barrier, peers)

    def part(t):
        return pl.ds(pl.multiple_of(t * rows, rows), rows)

    def copy(source, block, t, side):
        da, db = sides[side]
        return pltpu.make_async_remote_copy(
            src_ref=source,
            dst_ref=full_ref.at[block, part(t)],
            send_sem=send_sem.at[side, block, t],
            recv_sem=recv_sem.at[block, t],
            device_id=(row, place(da, db)),
            device_id_type=MESH,
        )

    def keep(t):
        return pltpu.make_async_copy(own_ref.at[part(t)], full_ref.at[col, part(t)], local_sem.at[t])

    def targets(da, db, t):
        late = t >= first
        early = t < first
        chosen = []
        for side, (sa, sb) in enumerate(sides):
            if da == 0 and db == 0:
                use = inside(sa, sb)
            elif sa != 0:
                if da * sa > 0:
                    continue
                if da == 0:
                    use = inside(sa, sb) & late
                elif db == 0:
                    use = inside(sa, sb)
                else:
                    use = inside(sa, sb) & late
            else:
                if db * sb > 0:
                    continue
                if db == 0:
                    use = inside(sa, sb) & early
                elif da == 0:
                    use = inside(sa, sb)
                else:
                    use = inside(sa, sb) & early
            chosen.append((side, use))
        return chosen

    @pl.loop(0, tiles)
    def _(t):
        for side, use in targets(0, 0, t):

            @pl.when(use)
            def _(side=side):
                copy(own_ref.at[part(t)], col, t, side).start()

        keep(t).start()

    offsets = sorted(
        (
            (da, db)
            for da in range(1 - outer, outer)
            for db in range(1 - inner, inner)
            if (da, db) != (0, 0)
        ),
        key=lambda o: (abs(o[0]) + abs(o[1]), o),
    )
    far = outer + inner - 2
    for distance in range(1, far + 1):
        ring = [o for o in offsets if abs(o[0]) + abs(o[1]) == distance]

        @pl.loop(0, tiles)
        def _(t, ring=ring):
            for da, db in ring:

                @pl.when(inside(da, db))
                def _(da=da, db=db):
                    block = place(da, db)
                    landed = full_ref.at[block, part(t)]
                    copy(landed, block, t, 0).wait_recv()
                    for side, use in targets(da, db, t):

                        @pl.when(use)
                        def _(side=side):
                            copy(landed, block, t, side).start()

    @pl.loop(0, tiles)
    def _(t):
        keep(t).wait()
        for side, use in targets(0, 0, t):

            @pl.when(use)
            def _(side=side):
                copy(own_ref.at[part(t)], col, t, side).wait_send()

        for da, db in offsets:

            @pl.when(inside(da, db))
            def _(da=da, db=db):
                block = place(da, db)
                for side, use in targets(da, db, t):

                    @pl.when(use)
                    def _(side=side):
                        copy(full_ref.at[block, part(t)], block, t, side).wait_send()


def gather_columns(own, outer, inner, tiles):
    blocks = outer * inner
    rows = own.shape[0] // tiles
    first = tiles - max(1, round(tiles / 6))
    return pl.pallas_call(
        functools.partial(gather_kernel, outer, inner, tiles, first, rows),
        out_shape=jax.ShapeDtypeStruct((blocks,) + own.shape, own.dtype),
        in_specs=[pl.BlockSpec(memory_space=pl.ANY)],
        out_specs=pl.BlockSpec(memory_space=pl.ANY),
        scratch_shapes=[
            pltpu.SemaphoreType.DMA((4, blocks, tiles)),
            pltpu.SemaphoreType.DMA((blocks, tiles)),
            pltpu.SemaphoreType.DMA((tiles,)),
        ],
        compiler_params=pltpu.CompilerParams(collective_id=0, has_side_effects=True),
        cost_estimate=pl.CostEstimate(flops=0, bytes_accessed=700_000_000, transcendentals=0),
    )(own)


def update_kernel(blocks, fold, full_ref, solved_ref, mine_ref, rhs_ref, out_ref, high_ref, low_ref):
    step = pl.program_id(0)
    width = full_ref.shape[2] // fold
    piece = width // PANELS
    rows = full_ref.shape[1]

    @pl.when(step == 0)
    def _():
        for c in range(blocks):
            for p in range(PANELS):
                x = solved_ref[p * PANEL + c * piece : p * PANEL + (c + 1) * piece, :]
                high = x.astype(jnp.bfloat16)
                at = c * width + p * piece
                high_ref[at : at + piece, :] = high
                low_ref[at : at + piece, :] = (x - high.astype(jnp.float32)).astype(jnp.bfloat16)
        out_ref[...] = mine_ref[...]

    @pl.when(step > 0)
    def _():
        halves = []
        for h in range(fold):
            halves.append(
                jnp.concatenate(
                    [full_ref[c, :, h * width : (h + 1) * width] for c in range(blocks)], axis=1
                )
            )
        left = jnp.concatenate(halves, axis=0)
        high = left.astype(jnp.bfloat16)
        low = (left - high.astype(jnp.float32)).astype(jnp.bfloat16)
        dot = functools.partial(jnp.dot, preferred_element_type=jnp.float32)
        total = dot(high, low_ref[...]) + dot(low, high_ref[...])
        total = total + dot(high, high_ref[...])
        out_ref[...] = rhs_ref[...] - total


def update_rows(full, solved, mine, rhs, fold, tiles):
    blocks, packed, lanes = full.shape
    tile = mine.shape[0]
    columns = rhs.shape[1]
    rows = packed // tiles
    window = solved.shape[0]
    return pl.pallas_call(
        functools.partial(update_kernel, blocks, fold),
        grid=(tiles + 1,),
        out_shape=jax.ShapeDtypeStruct(rhs.shape, rhs.dtype),
        in_specs=[
            pl.BlockSpec((blocks, rows, lanes), lambda i: (0, jnp.maximum(i - 1, 0), 0)),
            pl.BlockSpec((window, columns), lambda i: (0, 0)),
            pl.BlockSpec((tile, columns), lambda i: (0, 0)),
            pl.BlockSpec((tile, columns), lambda i: (i, 0)),
        ],
        out_specs=pl.BlockSpec((tile, columns), lambda i: (i, 0)),
        scratch_shapes=[
            pltpu.VMEM((window, columns), jnp.bfloat16),
            pltpu.VMEM((window, columns), jnp.bfloat16),
        ],
        compiler_params=pltpu.CompilerParams(vmem_limit_bytes=60 * 1024 * 1024),
    )(full, solved, mine, rhs)


def invert_lower(blocks):
    size = blocks.shape[-1]
    r = lax.broadcasted_iota(jnp.int32, (size, size), 0)
    c = lax.broadcasted_iota(jnp.int32, (size, size), 1)
    multiply = functools.partial(
        jnp.einsum, "bij,bjk->bik", precision=HIGHEST, preferred_element_type=jnp.float32
    )
    inverse = jnp.where(r == c, 1.0 / jnp.where(r == c, blocks, 1.0), 0.0)
    width = 1
    while width < size:
        off = (r // (2 * width) == c // (2 * width)) & (r // width != c // width)
        inner = jnp.where(off, blocks, 0.0)
        inverse = inverse - multiply(multiply(inverse, inner), inverse)
        width *= 2
    return inverse


def local(rhs_tile, factor, inner):
    row_count = lax.axis_size("row")
    col_count = lax.axis_size("col")
    row_piece = PANEL // row_count
    col_piece = PANEL // col_count
    my_row = lax.axis_index("row")
    window = PANELS * row_piece
    rows, width = factor.shape
    columns = rhs_tile.shape[1]
    tiles = (rows - window) // window
    fold = 128 // math.gcd(width, 128)

    own = factor[window:].reshape(tiles, fold, window // fold, width)
    own = own.transpose(0, 2, 1, 3).reshape(tiles * window // fold, fold * width)

    strip = lax.all_gather(factor[:window], "col", axis=0)
    lower = lax.all_gather(strip, "row", axis=0)
    stacked = lax.all_gather(rhs_tile[:window], "row", axis=0)
    full = gather_columns(own, col_count // inner, inner, tiles)

    total = PANELS * PANEL
    lower = lower.reshape(row_count, col_count, PANELS, row_piece, PANELS, col_piece)
    lower = lower.transpose(2, 0, 3, 4, 1, 5).reshape(total, total)
    stacked = stacked.reshape(row_count, PANELS, row_piece, columns)
    stacked = stacked.transpose(1, 0, 2, 3).reshape(total, columns)
    diagonal = jnp.stack(
        [lower[p * PANEL : (p + 1) * PANEL, p * PANEL : (p + 1) * PANEL] for p in range(PANELS)]
    )
    inverse = invert_lower(diagonal)
    multiply = functools.partial(jnp.dot, precision=HIGHEST, preferred_element_type=jnp.float32)
    solved = multiply(inverse[0], stacked[:PANEL])
    for p in range(1, PANELS):
        at = p * PANEL
        rest = stacked[at : at + PANEL] - multiply(lower[at : at + PANEL, :at], solved)
        solved = jnp.concatenate([solved, multiply(inverse[p], rest)], axis=0)
    mine = lax.dynamic_slice_in_dim(
        solved.reshape(PANELS, PANEL, columns), my_row * row_piece, row_piece, 1
    ).reshape(window, columns)
    return update_rows(full, solved, mine, rhs_tile, fold, tiles)


def inner_size(mesh):
    count = mesh.shape["col"]
    try:
        where = [tuple(d.coords) for d in mesh.devices.reshape(-1, count)[0]]
        inner = 1
        while inner < count and sum(p != q for p, q in zip(where[inner], where[0])) == 1 and (
            inner == 1 or [p != q for p, q in zip(where[inner], where[0])]
            == [p != q for p, q in zip(where[1], where[0])]
        ):
            inner += 1
        if count % inner == 0:
            return inner
    except Exception:
        pass
    return 2 if count % 2 == 0 else 1


def solution(mesh):
    specs = P("row", "col")
    body = functools.partial(local, inner=inner_size(mesh))
    return jax.shard_map(body, mesh=mesh, in_specs=(specs, specs), out_specs=specs, check_vma=False)
```

```python
import functools
import math

import jax
import jax.numpy as jnp
from jax import lax
from jax.experimental import pallas as pl
from jax.experimental.pallas import tpu as pltpu
from jax.sharding import PartitionSpec as P

PANEL = 512
PANELS = 3
HIGHEST = lax.Precision.HIGHEST
MESH = pl.DeviceIdType.MESH


def gather_kernel(
    outer, inner, peers, tiles, first, rows,
    own_ref, full_ref, window_ref, send_sem, recv_sem, local_sem, push_sem, pull_sem, stay_sem,
):
    row = lax.axis_index("row")
    col = lax.axis_index("col")
    a, b = lax.div(col, inner), lax.rem(col, inner)
    sides = ((1, 0), (-1, 0), (0, 1), (0, -1))

    def inside(da, db):
        return (a + da >= 0) & (a + da < outer) & (b + db >= 0) & (b + db < inner)

    def place(da, db):
        return (a + da) * inner + b + db

    barrier = pltpu.get_barrier_semaphore()
    for da, db in sides:

        @pl.when(inside(da, db))
        def _(da=da, db=db):
            pl.semaphore_signal(barrier, inc=1, device_id=(row, place(da, db)), device_id_type=MESH)

    for k in range(1, peers):
        pl.semaphore_signal(
            barrier, inc=1, device_id=(lax.rem(row + k, peers), col), device_id_type=MESH
        )
    near = sum(inside(da, db).astype(jnp.int32) for da, db in sides)
    pl.semaphore_wait(barrier, near + peers - 1)

    def part(t):
        return pl.ds(pl.multiple_of(t * rows, rows), rows)

    def copy(source, block, t, side):
        da, db = sides[side]
        return pltpu.make_async_remote_copy(
            src_ref=source,
            dst_ref=full_ref.at[block, part(t)],
            send_sem=send_sem.at[side, block, t],
            recv_sem=recv_sem.at[block, t],
            device_id=(row, place(da, db)),
            device_id_type=MESH,
        )

    def keep(t):
        return pltpu.make_async_copy(own_ref.at[part(t)], full_ref.at[col, part(t)], local_sem.at[t])

    def targets(da, db, t):
        late = t >= first
        early = t < first
        chosen = []
        for side, (sa, sb) in enumerate(sides):
            if da == 0 and db == 0:
                use = inside(sa, sb)
            elif sa != 0:
                if da * sa > 0:
                    continue
                if da == 0:
                    use = inside(sa, sb) & late
                elif db == 0:
                    use = inside(sa, sb)
                else:
                    use = inside(sa, sb) & late
            else:
                if db * sb > 0:
                    continue
                if db == 0:
                    use = inside(sa, sb) & early
                elif da == 0:
                    use = inside(sa, sb)
                else:
                    use = inside(sa, sb) & early
            chosen.append((side, use))
        return chosen

    def launch(t):
        for side, use in targets(0, 0, t):

            @pl.when(use)
            def _(side=side):
                copy(own_ref.at[part(t)], col, t, side).start()

        keep(t).start()

    def push(k, c, sender):
        return pltpu.make_async_remote_copy(
            src_ref=full_ref.at[c, part(0)],
            dst_ref=window_ref.at[sender, c],
            send_sem=push_sem.at[k, c],
            recv_sem=pull_sem.at[sender, c],
            device_id=(lax.rem(row + k, peers), col),
            device_id_type=MESH,
        )

    def stay(c):
        return pltpu.make_async_copy(full_ref.at[c, part(0)], window_ref.at[row, c], stay_sem.at[c])

    lead = min(3, tiles)
    pl.loop(0, lead)(launch)

    offsets = sorted(
        (
            (da, db)
            for da in range(1 - outer, outer)
            for db in range(1 - inner, inner)
            if (da, db) != (0, 0)
        ),
        key=lambda o: (abs(o[0]) + abs(o[1]), o),
    )
    far = outer + inner - 2
    rings = [[o for o in offsets if abs(o[0]) + abs(o[1]) == d] for d in range(1, far + 1)]

    def pass_on(t, ring):
        for da, db in ring:

            @pl.when(inside(da, db))
            def _(da=da, db=db):
                block = place(da, db)
                landed = full_ref.at[block, part(t)]
                copy(landed, block, t, 0).wait_recv()
                for side, use in targets(da, db, t):

                    @pl.when(use)
                    def _(side=side):
                        copy(landed, block, t, side).start()

    for ring in rings:
        pl.loop(0, 1)(functools.partial(pass_on, ring=ring))
    pl.loop(lead, tiles)(launch)
    keep(0).wait()

    @pl.loop(0, outer * inner)
    def _(c):
        for k in range(1, peers):
            push(k, c, row).start()
        stay(c).start()

    for ring in rings:
        pl.loop(1, tiles)(functools.partial(pass_on, ring=ring))

    @pl.loop(0, outer * inner)
    def _(c):
        stay(c).wait()
        for k in range(1, peers):
            push(k, c, row).wait_send()
            push(k, c, lax.rem(row + peers - k, peers)).wait_recv()

    @pl.loop(1, tiles)
    def _(t):
        keep(t).wait()

    @pl.loop(0, tiles)
    def _(t):
        for side, use in targets(0, 0, t):

            @pl.when(use)
            def _(side=side):
                copy(own_ref.at[part(t)], col, t, side).wait_send()

        for da, db in offsets:

            @pl.when(inside(da, db))
            def _(da=da, db=db):
                block = place(da, db)
                for side, use in targets(da, db, t):

                    @pl.when(use)
                    def _(side=side):
                        copy(full_ref.at[block, part(t)], block, t, side).wait_send()


def gather_columns(own, outer, inner, peers, tiles):
    blocks = outer * inner
    rows = own.shape[0] // tiles
    first = tiles - max(1, round(tiles / 6))
    return pl.pallas_call(
        functools.partial(gather_kernel, outer, inner, peers, tiles, first, rows),
        out_shape=[
            jax.ShapeDtypeStruct((blocks,) + own.shape, own.dtype),
            jax.ShapeDtypeStruct((peers, blocks, rows, own.shape[1]), own.dtype),
        ],
        in_specs=[pl.BlockSpec(memory_space=pl.ANY)],
        out_specs=[pl.BlockSpec(memory_space=pl.ANY)] * 2,
        scratch_shapes=[
            pltpu.SemaphoreType.DMA((4, blocks, tiles)),
            pltpu.SemaphoreType.DMA((blocks, tiles)),
            pltpu.SemaphoreType.DMA((tiles,)),
            pltpu.SemaphoreType.DMA((peers, blocks)),
            pltpu.SemaphoreType.DMA((peers, blocks)),
            pltpu.SemaphoreType.DMA((blocks,)),
        ],
        compiler_params=pltpu.CompilerParams(collective_id=0, has_side_effects=True),
        cost_estimate=pl.CostEstimate(flops=0, bytes_accessed=700_000_000, transcendentals=0),
    )(own)


def invert_lower(block):
    size = block.shape[-1]
    r = lax.broadcasted_iota(jnp.int32, (size, size), 0)
    c = lax.broadcasted_iota(jnp.int32, (size, size), 1)
    inverse = jnp.where(r == c, 1.0 / jnp.where(r == c, block, 1.0), 0.0)
    shift = 0
    while (1 << shift) < size:
        off = ((r >> (shift + 1)) == (c >> (shift + 1))) & ((r >> shift) != (c >> shift))
        inner = jnp.where(off, block, 0.0)
        inverse = inverse - exact(exact(inverse, inner), inverse)
        shift += 1
    return inverse


def exact(x, y):
    return jnp.dot(x, y, precision=HIGHEST, preferred_element_type=jnp.float32)


def solve(window_ref, strip_ref, strip_sem, lower_ref, x_ref, inverse_ref):
    peers, blocks, rows, lanes = window_ref.shape
    own = x_ref.shape[0] // peers
    fold = own // rows
    width = lanes // fold
    piece = width // PANELS
    row_piece = PANEL // peers

    def fetch(r):
        return pltpu.make_async_copy(window_ref.at[r], strip_ref, strip_sem.at[r % 2])

    for r in range(peers):
        fetch(r).start()
        fetch(r).wait()
        for h in range(fold):
            at = r * own + h * rows
            for p in range(PANELS):
                left = h * width + p * piece
                lower_ref[p, at : at + rows, :] = jnp.concatenate(
                    [strip_ref[c, :, left : left + piece] for c in range(blocks)], axis=1
                )
    groups = [(p, r) for p in range(PANELS) for r in range(peers)]

    @pl.loop(0, PANELS)
    def _(p):
        for r in range(peers):
            at = pl.multiple_of(r * own + p * row_piece, row_piece)
            block = lower_ref[p, pl.ds(at, row_piece), r * row_piece : (r + 1) * row_piece]
            inverse_ref[p * peers + r] = invert_lower(block)

    for p, r in groups:
        at = r * own + p * row_piece
        here = p * PANEL + r * row_piece
        rest = x_ref[here : here + row_piece, :]
        for q in range(p):
            rest = rest - exact(
                lower_ref[q, at : at + row_piece, :], x_ref[q * PANEL : (q + 1) * PANEL, :]
            )
        if r > 0:
            rest = rest - exact(
                lower_ref[p, at : at + row_piece, : r * row_piece], x_ref[p * PANEL : here, :]
            )
        x_ref[here : here + row_piece, :] = exact(inverse_ref[p * peers + r], rest)


def update_kernel(
    full_ref, window_ref, stacked_ref, rhs_ref, out_ref, high_ref, low_ref, lower_ref, x_ref, inverse_ref, load_sem,
    strip_ref, strip_sem,
):
    step = pl.program_id(0)
    peers, blocks, rows, lanes = window_ref.shape
    tile = out_ref.shape[0]
    fold = tile // rows
    width = lanes // fold
    piece = width // PANELS
    row_piece = PANEL // peers

    @pl.when(step == 0)
    def _():
        copies = [
            pltpu.make_async_copy(
                stacked_ref.at[r, pl.ds(p * row_piece, row_piece)],
                x_ref.at[pl.ds(p * PANEL + r * row_piece, row_piece)],
                load_sem.at[p, r],
            )
            for p in range(PANELS)
            for r in range(peers)
        ]
        for one in copies:
            one.start()
        for one in copies:
            one.wait()
        solve(window_ref, strip_ref, strip_sem, lower_ref, x_ref, inverse_ref)
        for c in range(blocks):
            for p in range(PANELS):
                x = x_ref[p * PANEL + c * piece : p * PANEL + (c + 1) * piece, :]
                high = x.astype(jnp.bfloat16)
                at = c * width + p * piece
                high_ref[at : at + piece, :] = high
                low_ref[at : at + piece, :] = (x - high.astype(jnp.float32)).astype(jnp.bfloat16)
        mine = lax.axis_index("row") * row_piece
        for p in range(PANELS):
            at = pl.multiple_of(p * PANEL + mine, row_piece)
            out_ref[p * row_piece : (p + 1) * row_piece, :] = x_ref[pl.ds(at, row_piece), :]

    @pl.when(step > 0)
    def _():
        halves = []
        for h in range(fold):
            halves.append(
                jnp.concatenate(
                    [full_ref[c, :, h * width : (h + 1) * width] for c in range(blocks)], axis=1
                )
            )
        left = jnp.concatenate(halves, axis=0)
        high = left.astype(jnp.bfloat16)
        low = (left - high.astype(jnp.float32)).astype(jnp.bfloat16)
        dot = functools.partial(jnp.dot, preferred_element_type=jnp.float32)
        columns = out_ref.shape[1]
        part = columns // 3 if columns % 384 == 0 else columns

        @pl.loop(0, columns // part)
        def _(n):
            at = pl.ds(pl.multiple_of(n * part, part), part)
            total = dot(high, low_ref[:, at]) + dot(low, high_ref[:, at])
            total = total + dot(high, high_ref[:, at])
            out_ref[:, at] = rhs_ref[:, at] - total


def update_rows(full, window, stacked, rhs, tiles):
    blocks, packed, lanes = full.shape
    peers, _, rows, _ = window.shape
    tile = stacked.shape[1]
    columns = rhs.shape[1]
    total = peers * tile
    row_piece = PANEL // peers
    return pl.pallas_call(
        update_kernel,
        grid=(tiles,),
        out_shape=jax.ShapeDtypeStruct(rhs.shape, rhs.dtype),
        in_specs=[
            pl.BlockSpec((blocks, rows, lanes), lambda i: (0, i, 0)),
            pl.BlockSpec(memory_space=pl.ANY),
            pl.BlockSpec(memory_space=pl.ANY),
            pl.BlockSpec((tile, columns), lambda i: (i, 0)),
        ],
        out_specs=pl.BlockSpec((tile, columns), lambda i: (i, 0)),
        scratch_shapes=[
            pltpu.VMEM((total, columns), jnp.bfloat16),
            pltpu.VMEM((total, columns), jnp.bfloat16),
            pltpu.VMEM((PANELS, total, PANEL), jnp.float32),
            pltpu.VMEM((total, columns), jnp.float32),
            pltpu.VMEM((PANELS * peers, row_piece, row_piece), jnp.float32),
            pltpu.SemaphoreType.DMA((PANELS, peers)),
            pltpu.VMEM((blocks, rows, lanes), jnp.float32),
            pltpu.SemaphoreType.DMA((2,)),
        ],
        compiler_params=pltpu.CompilerParams(vmem_limit_bytes=67_043_328),
    )(full, window, stacked, rhs)


def local(rhs_tile, factor, inner):
    row_count = lax.axis_size("row")
    col_count = lax.axis_size("col")
    window = PANELS * (PANEL // row_count)
    rows, width = factor.shape
    tiles = rows // window
    fold = 128 // math.gcd(width, 128)

    own = factor.reshape(tiles, fold, window // fold, width)
    own = own.transpose(0, 2, 1, 3).reshape(rows // fold, fold * width)
    stacked = lax.all_gather(rhs_tile[:window], "row", axis=0)
    full, strips = gather_columns(own, col_count // inner, inner, row_count, tiles)
    return update_rows(full, strips, stacked, rhs_tile, tiles)


def inner_size(mesh):
    count = mesh.shape["col"]
    try:
        where = [tuple(d.coords) for d in mesh.devices.reshape(-1, count)[0]]
        inner = 1
        while inner < count and sum(p != q for p, q in zip(where[inner], where[0])) == 1 and (
            inner == 1 or [p != q for p, q in zip(where[inner], where[0])]
            == [p != q for p, q in zip(where[1], where[0])]
        ):
            inner += 1
        if count % inner == 0:
            return inner
    except Exception:
        pass
    return 2 if count % 2 == 0 else 1


def solution(mesh):
    specs = P("row", "col")
    body = functools.partial(local, inner=inner_size(mesh))
    return jax.shard_map(body, mesh=mesh, in_specs=(specs, specs), out_specs=specs, check_vma=False)
```
